256 devices in a mesh: rep: 16 (over z_lo, x), tp: 16 (over z_hi, y, core).
Axes of the slice: x: 4, y: 4, z: 8 (z_hi: 2, z_lo: 4; z = z_hi * 4 + z_lo), core: 2. Of those that a mesh axis runs over, the one named last changes fastest.
Arguments:
- tokens: bfloat16 [8192, 4096], P('rep'), may hold values from -6 to 6
- cotangent: bfloat16 [8192, 4096], P('rep'), may hold values from -6 to 6
- token_ids: int32 [8192], P('rep'), may hold values from 0 to 128255, as said below
- partner: int32 [16], replicated, may hold values from 0 to 15, as said below
- gate_up: bfloat16 [2, 4096, 14336], P(None, 'rep', 'tp'), may hold values from -0.09375 to 0.09375
- down: bfloat16 [14336, 4096], P('tp', 'rep'), may hold values from -0.046875 to 0.046875
- wide_side: float32 [16, 3, 64, 4096], P('rep', None, None, 'tp'), may hold values from -6 to 6
- hidden_side: float32 [16, 3, 64, 14336], P('rep', None, None, 'tp'), may hold values from -6 to 6
- wide_mom: float32 [16, 3, 64, 4096], P('rep', None, None, 'tp'), may hold values from -4 to 4
- hidden_mom: float32 [16, 3, 64, 14336], P('rep', None, None, 'tp'), may hold values from -4 to 4
- wide_var: float32 [16, 3, 64, 4096], P('rep', None, None, 'tp'), may hold values from 0.01 to 1
- hidden_var: float32 [16, 3, 64, 14336], P('rep', None, None, 'tp'), may hold values from 0.01 to 1
Outputs:
- new_wide: float32 [16, 3, 64, 4096], P('rep', None, None, 'tp')
- new_hidden: float32 [16, 3, 64, 14336], P('rep', None, None, 'tp')
- new_wide_mom: float32 [16, 3, 64, 4096], P('rep', None, None, 'tp')
- new_hidden_mom: float32 [16, 3, 64, 14336], P('rep', None, None, 'tp')
- new_wide_var: float32 [16, 3, 64, 4096], P('rep', None, None, 'tp')
- new_hidden_var: float32 [16, 3, 64, 14336], P('rep', None, None, 'tp')
- wide_copy: bfloat16 [16, 3, 64, 4096], P('rep')
The draws below stay inside these ranges and needn't reach their ends.
Inputs may be any that keep to these rules, and one draw needn't show every extreme that they name: `token_ids`: in each replica's block of 512 positions the ids are nonzero up to that replica's length and 0 after it; lengths lie between 128 and 512, some replica has no padding and another has length 128. There is one k, 1 <= k < 16, such that partner[r] is r XOR k or r itself for every r; partner[partner[r]] = r.
All inputs are finite; a program needn't handle non-finite values.
Results may differ from the reference program's by a relative error of at most 0.014.
Values may be sent and summed in bfloat16 or wider, within the bound.
No kernel may reach another device: no remote copies, remote signals or barrier semaphores. Data moves between devices by JAX's collectives and lax.ppermute only.
A program may use at most 128 MiB of HBM per device.

```python
import math
import jax
import jax.numpy as jnp
from jax import lax

D = 4096
FF = 14336
R = 64
VOCAB = 128256
TOK = 512
TOKENS = 8192
N_REP = 16


def draw_token_ids(key, part):
    key_len = jax.random.fold_in(key, 11)
    key_full = jax.random.fold_in(key, 12)
    key_short = jax.random.fold_in(key, 13)
    key_ids = jax.random.fold_in(key, 14)
    lengths = jax.random.randint(key_len, (N_REP,), TOK // 4, TOK + 1)
    full_index = jax.random.randint(key_full, (), 0, N_REP)
    short_index = (full_index + jax.random.randint(key_short, (), 1, N_REP)) % N_REP
    lengths = lengths.at[full_index].set(TOK)
    lengths = lengths.at[short_index].set(TOK // 4)
    values = jax.random.randint(key_ids, (N_REP, TOK), 1, VOCAB)
    position = jnp.arange(TOK, dtype=jnp.int32)[None, :]
    values = jnp.where(position < lengths[:, None], values, 0)
    return values.reshape(N_REP * TOK).astype(jnp.int32)


def draw_partner(key, part):
    key_shift = jax.random.fold_in(key, 21)
    key_alive = jax.random.fold_in(key, 22)
    shift_value = jax.random.randint(key_shift, (), 1, N_REP)
    alive = jax.random.randint(key_alive, (N_REP,), 0, 4) > 0
    own = jnp.arange(N_REP, dtype=jnp.int32)
    other = jnp.bitwise_xor(own, shift_value)
    both = jnp.logical_and(alive, alive[other])
    return jnp.where(both, other, own).astype(jnp.int32)


def block_levels(key, extent, shards, low, top_value):
    loudness, own = 1.0, jax.random.fold_in(key, 6)
    for dim, blocks in shards:
        draws = jnp.exp(jax.random.uniform(jax.random.fold_in(own, dim), (blocks,), jnp.float32, low / len(shards), top_value / len(shards)))
        loudness = loudness * jnp.repeat(draws, extent[dim] // blocks).reshape([-1 if axis == dim else 1 for axis in range(len(extent))])
    return loudness


def noise(stream_key, extent, scale, reach, pieces=(), kind=jnp.bfloat16):
    drawn = scale * jax.random.normal(stream_key, extent, jnp.float32)
    if pieces:
        drawn = drawn * block_levels(stream_key, extent, pieces, -0.22, 0.18)
    return jnp.clip(drawn, -reach, reach).astype(kind)


def setup_inputs(seed: int = 0) -> dict:
    splits = jax.random.split(jax.random.key(seed), 13)
    return {
        "tokens": noise(splits[0], (TOKENS, D), 1.0, 6.0, ((0, 16),)),
        "cotangent": noise(splits[1], (TOKENS, D), 1.0, 6.0, ((0, 16),)),
        "token_ids": draw_token_ids(jax.random.fold_in(splits[12], 71), 0),
        "partner": draw_partner(jax.random.fold_in(splits[12], 71), 0),
        "gate_up": noise(splits[4], (2, D, FF), D ** -0.5, 0.09375, ((1, 16), (2, 16))),
        "down": noise(splits[5], (FF, D), FF ** -0.5, 0.046875, ((0, 16), (1, 16))),
        "wide_side": noise(splits[6], (N_REP, 3, R, D), 1.0, 6.0, ((0, 16), (3, 16)), jnp.float32),
        "hidden_side": noise(splits[7], (N_REP, 3, R, FF), 1.0, 6.0, ((0, 16), (3, 16)), jnp.float32),
        "wide_mom": noise(splits[8], (N_REP, 3, R, D), 0.3, 4.0, ((0, 16), (3, 16)), jnp.float32),
        "hidden_mom": noise(splits[9], (N_REP, 3, R, FF), 0.3, 4.0, ((0, 16), (3, 16)), jnp.float32),
        "wide_var": jnp.clip(jnp.exp(math.log(1.0) - 4.6051702 * jax.random.uniform(splits[10], (N_REP, 3, R, D), jnp.float32) ** block_levels(splits[10], (N_REP, 3, R, D), ((0, 16), (3, 16)), -0.2, 0.2)), 0.01, 1.0),
        "hidden_var": jnp.clip(jnp.exp(math.log(1.0) - 4.6051702 * jax.random.uniform(splits[11], (N_REP, 3, R, FF), jnp.float32) ** block_levels(splits[11], (N_REP, 3, R, FF), ((0, 16), (3, 16)), -0.2, 0.2)), 0.01, 1.0),
    }


adapter_scale = 0.5
learn_rate = 0.1
beta_one = 0.9
beta_two = 0.99
bias_one = 1.0 - 0.9 ** 10
bias_two = 1.0 - 0.99 ** 10
adam_eps = 1e-08

def adam_step(param, moment, second, grad):
    moment_new = beta_one * moment + (1.0 - beta_one) * grad
    second_new = beta_two * second + (1.0 - beta_two) * grad * grad
    param_new = param - learn_rate * (moment_new / bias_one) / (jnp.sqrt(second_new / bias_two) + adam_eps)
    return (param_new, moment_new, second_new)

def reference(tokens, cotangent, token_ids, partner, gate_up, down, wide_side, hidden_side, wide_mom, hidden_mom, wide_var, hidden_var):
    scale_left = 1.0 / math.sqrt(D)
    scale_right = 1.0 / math.sqrt(R)
    scale_down = 1.0 / math.sqrt(FF)
    toks = tokens.reshape(N_REP, TOK, D)
    cots = cotangent.reshape(N_REP, TOK, D)
    idss = token_ids.reshape(N_REP, TOK)

    def replica(items):
        input_rows, grads_out, ids, wide, hid, wmom, hmom, wvar, hvar = items
        wide_b = wide.astype(jnp.bfloat16)
        hidden_right = hid.astype(jnp.bfloat16)
        frozen_gate_weight = jnp.dot(input_rows, gate_up[0], preferred_element_type=jnp.float32)
        frozen_up_weight = jnp.dot(input_rows, gate_up[1], preferred_element_type=jnp.float32)
        pair_a = wide_b[:2].reshape(2 * R, D)
        low = (jnp.dot(input_rows, pair_a.T, preferred_element_type=jnp.float32) * scale_left).astype(jnp.bfloat16)
        gate_adapter_update = low[:, :R]
        up_adapter_update = low[:, R:]
        gate_values = frozen_gate_weight + adapter_scale * scale_right * jnp.dot(gate_adapter_update, hidden_right[0], preferred_element_type=jnp.float32)
        upper_bound = frozen_up_weight + adapter_scale * scale_right * jnp.dot(up_adapter_update, hidden_right[1], preferred_element_type=jnp.float32)
        sig = jax.nn.sigmoid(gate_values)
        act = gate_values * sig
        hidden_state = (act * upper_bound).astype(jnp.bfloat16)
        live = ids != 0
        masked_values = jnp.where(live[:, None], grads_out, jnp.zeros_like(grads_out))
        down_adapter_left = hidden_right[2]
        down_b = wide_b[2]
        up_down_right = (jnp.dot(hidden_state, down_adapter_left.T, preferred_element_type=jnp.float32) * scale_down).astype(jnp.bfloat16)
        weight_right = jnp.dot(masked_values, down_b.T, preferred_element_type=jnp.float32).astype(jnp.bfloat16)
        hidden_gradient = jnp.dot(masked_values, down.T, preferred_element_type=jnp.float32)
        hidden_gradient = hidden_gradient + adapter_scale * scale_down * scale_right * jnp.dot(weight_right, down_adapter_left, preferred_element_type=jnp.float32)
        gate_gradient = (hidden_gradient * upper_bound * sig * (1.0 + gate_values * (1.0 - sig))).astype(jnp.bfloat16)
        up_gradient = (hidden_gradient * act).astype(jnp.bfloat16)
        gradient_gate_right = adapter_scale * scale_right * jnp.dot(gate_adapter_update.T, gate_gradient, preferred_element_type=jnp.float32)
        gradient_up_right = adapter_scale * scale_right * jnp.dot(up_adapter_update.T, up_gradient, preferred_element_type=jnp.float32)
        gradient_down_left = adapter_scale * scale_down * scale_right * jnp.dot(weight_right.T, hidden_state, preferred_element_type=jnp.float32)
        gradient_down_right = adapter_scale * scale_right * jnp.dot(up_down_right.T, masked_values, preferred_element_type=jnp.float32)
        activation_product = jnp.concatenate([jnp.dot(gate_gradient, hidden_right[0].T, preferred_element_type=jnp.float32), jnp.dot(up_gradient, hidden_right[1].T, preferred_element_type=jnp.float32)], axis=1)
        gradient_left = adapter_scale * scale_left * scale_right * jnp.dot(activation_product.T, input_rows.astype(jnp.float32), precision=lax.Precision.HIGHEST)
        grad_wide = jnp.concatenate([gradient_left.reshape(2, R, D), gradient_down_right[None]], axis=0)
        grad_hid = jnp.stack([gradient_gate_right, gradient_up_right, gradient_down_left], axis=0)
        wide_new, wmom_new, wvar_new = adam_step(wide, wmom, wvar, grad_wide)
        hid_new, hmom_new, hvar_new = adam_step(hid, hmom, hvar, grad_hid)
        return (wide_new, hid_new, wmom_new, hmom_new, wvar_new, hvar_new)
    wide_new, hid_new, wmom_new, hmom_new, wvar_new, hvar_new = lax.map(replica, (toks, cots, idss, wide_side, hidden_side, wide_mom, hidden_mom, wide_var, hidden_var))
    own = jnp.arange(N_REP, dtype=jnp.int32)
    paired = (partner != own)[:, None, None, None]
    wide_final = jnp.where(paired, 0.5 * (wide_new + wide_new[partner]), wide_new)
    hid_final = jnp.where(paired, 0.5 * (hid_new + hid_new[partner]), hid_new)
    return (wide_final, hid_final, wmom_new, hmom_new, wvar_new, hvar_new, wide_final.astype(jnp.bfloat16))
```

```python
import math

import jax
import jax.numpy as jnp
from jax import lax
from jax.sharding import PartitionSpec as P


adapter_scale = 0.5
learn_rate = 0.1
beta_one = 0.9
beta_two = 0.99
bias_one = 1.0 - 0.9**10
bias_two = 1.0 - 0.99**10
adam_eps = 1e-08

BF = jnp.bfloat16
F32 = jnp.float32


def rep_xor(value, mask):
    return lax.ppermute(value, "rep", [(r, r ^ mask) for r in range(16)])


def rep_xshift(value, step):
    return lax.ppermute(value, "rep", [(r, (r & 12) | ((r + step) & 3)) for r in range(16)])


def tp_xor(value, mask):
    return lax.ppermute(value, "tp", [(t, t ^ mask) for t in range(16)])


def tp_yshift(value, step):
    return lax.ppermute(
        value, "tp", [(t, (t & 9) | ((((t >> 1) + step) & 3) << 1)) for t in range(16)]
    )


def adam_step(param, moment, second, grad):
    moment_new = beta_one * moment + (1.0 - beta_one) * grad
    second_new = beta_two * second + (1.0 - beta_two) * grad * grad
    param_new = param - learn_rate * (moment_new / bias_one) / (
        jnp.sqrt(second_new / bias_two) + adam_eps
    )
    return (param_new, moment_new, second_new)


def contract_last(left, right):
    return lax.dot_general(
        left, right, (((1,), (1,)), ((), ())), preferred_element_type=F32
    )


def contract_leading(left, right):
    return lax.dot_general(
        left, right, (((0,), (0,)), ((), ())), preferred_element_type=F32
    )


def matmul(left, right):
    return jnp.dot(left, right, preferred_element_type=F32)


def tp_sum(part, y, wire):
    rows = part.shape[0] // 4
    part = part + tp_xor(part.astype(wire), 1).astype(F32)

    def quarter(index):
        return lax.dynamic_slice_in_dim(part, (index & 3) * rows, rows, 0)

    total = quarter(y)
    for step in (1, 3, 2):
        total = total + tp_yshift(quarter(y + step).astype(wire), step).astype(F32)
    total = (total + tp_xor(total.astype(wire), 8).astype(F32)).astype(wire)
    pieces = [total] + [tp_yshift(total, 4 - step) for step in (1, 2, 3)]
    joined = jnp.concatenate(pieces + pieces[:3], axis=0)
    return lax.dynamic_slice_in_dim(joined, ((4 - y) & 3) * rows, 4 * rows, 0)


def ring_gather(own, shift, axis):
    half = own.shape[axis] // 2
    right = shift(own, -1)
    left = shift(own, 1)
    far_first = shift(lax.slice_in_dim(left, 0, half, axis=axis), 1)
    far_second = shift(lax.slice_in_dim(right, half, 2 * half, axis=axis), -1)
    return right, left, far_first, far_second


def tp_gather(own, y, h):
    other = tp_xor(own, 8)
    low_half = jnp.where(h == 0, own, other)
    high_half = jnp.where(h == 0, other, own)
    both = jnp.stack([low_half, high_half], axis=2)
    pieces = [both] + [tp_yshift(both, 4 - step) for step in (1, 2, 3)]
    ring = jnp.stack(pieces + pieces[:3], axis=3)
    ring = lax.dynamic_slice_in_dim(ring, (4 - y) & 3, 4, 3)
    return ring


def shards(
    tokens,
    cotangent,
    token_ids,
    partner,
    gate_up,
    down,
    wide_side,
    hidden_side,
    wide_mom,
    hidden_mom,
    wide_var,
    hidden_var,
):
    width = tokens.shape[1]
    adapter_rank = wide_side.shape[2]
    portion = wide_side.shape[3]
    scale_left = 1.0 / math.sqrt(width)
    scale_right = 1.0 / math.sqrt(adapter_rank)
    ff_part = down.shape[0]
    half = ff_part // 2
    scale_down = 1.0 / math.sqrt(16 * ff_part)
    scale_b = adapter_scale * scale_right
    tp_index = lax.axis_index("tp")
    rep_index = lax.axis_index("rep")
    zlo, xi = rep_index >> 2, rep_index & 3
    h, y, core = tp_index >> 3, (tp_index >> 1) & 3, tp_index & 1
    side = zlo & 1

    weights = jnp.concatenate([jnp.swapaxes(gate_up, 1, 2), down[None]], axis=0)
    first, second = weights[:, :half], weights[:, half:]
    mine = jnp.where(side == 0, first, second)
    theirs = jnp.where(side == 0, second, first)
    pieces = [mine, rep_xor(theirs, 4)]
    pieces.append(rep_xor(mine, 8))
    pieces.append(rep_xor(pieces[1], 8))

    live = token_ids != 0
    masked = jnp.where(live[:, None], cotangent, jnp.zeros_like(cotangent))
    wide_cols = width // 8
    column = (tp_index & 7) * wide_cols

    def partner_rows(array):
        part = rep_xor(lax.dynamic_slice_in_dim(array, column, wide_cols, 1), 4)
        right, left, far_first, far_second = ring_gather(part, tp_yshift, 0)
        far = jnp.concatenate([far_first, far_second], axis=0)
        own_core = jnp.stack([part, right, far, left], axis=0)
        other_core = tp_xor(own_core, 1)
        even = jnp.where(core == 0, own_core, other_core)
        odd = jnp.where(core == 0, other_core, own_core)
        return jnp.concatenate([even, odd], axis=2)

    x_partner = partner_rows(tokens)
    masked_partner = partner_rows(masked)

    wide = wide_side[0]
    hid = hidden_side[0]
    wide_b = wide.astype(BF)
    hid_b = hid.astype(BF)
    hid_first, hid_second = hid_b[:, :, :half], hid_b[:, :, half:]
    hid_mine = jnp.where(side == 0, hid_first, hid_second)
    hid_pair = [hid_mine, rep_xor(jnp.where(side == 0, hid_second, hid_first), 4)]

    x_part = lax.dynamic_slice_in_dim(tokens, tp_index * portion, portion, 1)
    masked_part = lax.dynamic_slice_in_dim(masked, tp_index * portion, portion, 1)
    pair_a = wide_b[:2].reshape(2 * adapter_rank, portion)
    start = jnp.concatenate(
        [contract_last(x_part, pair_a), contract_last(masked_part, wide_b[2])], axis=1
    )
    start = tp_sum(start, y, F32)
    low_w = jnp.concatenate(
        [
            (start[:, : 2 * adapter_rank] * scale_left).astype(BF),
            start[:, 2 * adapter_rank :].astype(BF),
        ],
        axis=1,
    )
    low_w_pair = [low_w, rep_xor(low_w, 4)]

    sums = [[None] * 3, [None] * 3]
    for zoff in range(4):
        own = pieces[zoff]
        right, left, far_first, far_second = ring_gather(own, rep_xshift, 1)
        zero = jnp.int32(0)

        def place(buffer, piece, xoff, row):
            col = ((xi + xoff) & 3) * portion
            return lax.dynamic_update_slice(buffer, piece, (zero, jnp.int32(row), col))

        block = jnp.concatenate([own] * 4, axis=2)
        block = place(block, right, 1, 0)
        block = place(block, left, 3, 0)
        block = place(block, far_first, 2, 0)
        block = place(block, far_second, 2, half // 2)
        where_z = zlo ^ zoff
        where_p = (where_z - y) & 3
        rows = [
            [
                lax.dynamic_slice_in_dim(tokens, where_z * 4 * portion, 4 * portion, 1),
                lax.dynamic_slice_in_dim(masked, where_z * 4 * portion, 4 * portion, 1),
            ],
            [
                lax.dynamic_index_in_dim(x_partner, where_p, 0, keepdims=False),
                lax.dynamic_index_in_dim(masked_partner, where_p, 0, keepdims=False),
            ],
        ]
        for q in range(2):
            for k in range(3):
                term = contract_last(rows[q][k // 2], block[k])
                sums[q][k] = term if zoff == 0 else sums[q][k] + term

    partials, grads = [], []
    for q in range(2):
        low_gate = low_w_pair[q][:, :adapter_rank]
        low_up = low_w_pair[q][:, adapter_rank : 2 * adapter_rank]
        weight_right = low_w_pair[q][:, 2 * adapter_rank :]
        hid_q = hid_pair[q]
        gate_values = sums[q][0] + scale_b * matmul(low_gate, hid_q[0])
        up_values = sums[q][1] + scale_b * matmul(low_up, hid_q[1])
        hidden_gradient = sums[q][2] + scale_b * scale_down * matmul(weight_right, hid_q[2])
        sig = jax.nn.sigmoid(gate_values)
        act = gate_values * sig
        hidden_state = (act * up_values).astype(BF)
        gate_gradient = (
            hidden_gradient * up_values * sig * (1.0 + gate_values * (1.0 - sig))
        ).astype(BF)
        up_gradient = (hidden_gradient * act).astype(BF)
        partials.append(
            jnp.concatenate(
                [
                    contract_last(gate_gradient, hid_q[0]),
                    contract_last(up_gradient, hid_q[1]),
                    contract_last(hidden_state, hid_q[2]),
                ],
                axis=1,
            )
        )
        grads.append(
            jnp.stack(
                [
                    scale_b * contract_leading(low_gate, gate_gradient),
                    scale_b * contract_leading(low_up, up_gradient),
                    scale_b * scale_down * contract_leading(weight_right, hidden_state),
                ],
                axis=0,
            )
        )
    partial = partials[0] + rep_xor(partials[1].astype(BF), 4).astype(F32)
    summed = tp_sum(partial, y, BF)
    zsum = summed[:, : 2 * adapter_rank]
    ud = (summed[:, 2 * adapter_rank :].astype(F32) * scale_down).astype(BF)

    grad_other = rep_xor(grads[1].astype(BF), 4).astype(F32)
    grad_hid = jnp.where(
        side == 0,
        jnp.concatenate([grads[0], grad_other], axis=2),
        jnp.concatenate([grad_other, grads[0]], axis=2),
    )
    gradient_down_right = scale_b * contract_leading(ud, masked_part)
    gradient_left = (
        adapter_scale * scale_left * scale_right * contract_leading(zsum, x_part)
    ).reshape(2, adapter_rank, portion)
    grad_wide = jnp.concatenate([gradient_left, gradient_down_right[None]], axis=0)
    wide_new, wmom_new, wvar_new = adam_step(wide, wide_mom[0], wide_var[0], grad_wide)
    hid_new, hmom_new, hvar_new = adam_step(hid, hidden_mom[0], hidden_var[0], grad_hid)

    own_ids = jnp.arange(partner.shape[0], dtype=jnp.int32)
    shift_value = jnp.max(jnp.bitwise_xor(partner, own_ids))
    paired = partner[rep_index] != rep_index

    def swap(value):
        branches = [lambda v: v] + [
            (lambda v, mask=mask: rep_xor(v, mask)) for mask in range(1, 16)
        ]
        return lax.switch(shift_value, branches, value)

    def average(new, received):
        return jnp.where(paired, 0.5 * (new + received.astype(F32)), new)

    received_wide = swap(wide_new.astype(BF))
    hid_send, received_wide = lax.optimization_barrier((hid_new.astype(BF), received_wide))
    wide_final = average(wide_new, received_wide)
    hid_final = average(hid_new, swap(hid_send))

    ring = tp_gather(wide_final.astype(BF), y, h)
    other = tp_xor(ring, 1)
    even = jnp.where(core == 0, ring, other)
    odd = jnp.where(core == 0, other, ring)
    wide_copy = jnp.stack([even, odd], axis=4).reshape(3, adapter_rank, 16 * portion)
    return (
        wide_final[None],
        hid_final[None],
        wmom_new[None],
        hmom_new[None],
        wvar_new[None],
        hvar_new[None],
        wide_copy[None],
    )


def solution(mesh):
    side = P("rep", None, None, "tp")
    return jax.shard_map(
        shards,
        mesh=mesh,
        in_specs=(
            P("rep", None),
            P("rep", None),
            P("rep"),
            P(),
            P(None, "rep", "tp"),
            P("tp", "rep"),
            side,
            side,
            side,
            side,
            side,
            side,
        ),
        out_specs=(side, side, side, side, side, side, P("rep", None, None, None)),
        check_vma=False,
    )
```

```python
import math

import jax
import jax.numpy as jnp
from jax import lax
from jax.sharding import PartitionSpec as P


adapter_scale = 0.5
learn_rate = 0.1
beta_one = 0.9
beta_two = 0.99
bias_one = 1.0 - 0.9**10
bias_two = 1.0 - 0.99**10
adam_eps = 1e-08

BF = jnp.bfloat16
F32 = jnp.float32


def rep_xor(value, mask):
    return lax.ppermute(value, "rep", [(r, r ^ mask) for r in range(16)])


def rep_xshift(value, step):
    return lax.ppermute(value, "rep", [(r, (r & 12) | ((r + step) & 3)) for r in range(16)])


def tp_xor(value, mask):
    return lax.ppermute(value, "tp", [(t, t ^ mask) for t in range(16)])


def tp_yshift(value, step):
    return lax.ppermute(
        value, "tp", [(t, (t & 9) | ((((t >> 1) + step) & 3) << 1)) for t in range(16)]
    )


def adam_step(param, moment, second, grad):
    moment_new = beta_one * moment + (1.0 - beta_one) * grad
    second_new = beta_two * second + (1.0 - beta_two) * grad * grad
    param_new = param - learn_rate * (moment_new / bias_one) / (
        jnp.sqrt(second_new / bias_two) + adam_eps
    )
    return (param_new, moment_new, second_new)


def contract_last(left, right):
    return lax.dot_general(
        left, right, (((1,), (1,)), ((), ())), preferred_element_type=F32
    )


def contract_leading(left, right):
    return lax.dot_general(
        left, right, (((0,), (0,)), ((), ())), preferred_element_type=F32
    )


def matmul(left, right):
    return jnp.dot(left, right, preferred_element_type=F32)


def tp_sum(part, y, wire):
    rows = part.shape[0] // 4
    part = part + tp_xor(part.astype(wire), 1).astype(F32)

    def quarter(index):
        return lax.dynamic_slice_in_dim(part, (index & 3) * rows, rows, 0)

    total = quarter(y)
    for step in (1, 3, 2):
        total = total + tp_yshift(quarter(y + step).astype(wire), step).astype(F32)
    total = (total + tp_xor(total.astype(wire), 8).astype(F32)).astype(wire)
    pieces = [total] + [tp_yshift(total, 4 - step) for step in (1, 2, 3)]
    joined = jnp.concatenate(pieces + pieces[:3], axis=0)
    return lax.dynamic_slice_in_dim(joined, ((4 - y) & 3) * rows, 4 * rows, 0)


def ring_gather(own, shift, axis):
    half = own.shape[axis] // 2
    right = shift(own, -1)
    left = shift(own, 1)
    far_first = shift(lax.slice_in_dim(left, 0, half, axis=axis), 1)
    far_second = shift(lax.slice_in_dim(right, half, 2 * half, axis=axis), -1)
    return right, left, far_first, far_second


def shards(
    tokens,
    cotangent,
    token_ids,
    partner,
    gate_up,
    down,
    wide_side,
    hidden_side,
    wide_mom,
    hidden_mom,
    wide_var,
    hidden_var,
):
    width = tokens.shape[1]
    adapter_rank = wide_side.shape[2]
    portion = wide_side.shape[3]
    scale_left = 1.0 / math.sqrt(width)
    scale_right = 1.0 / math.sqrt(adapter_rank)
    ff_part = down.shape[0]
    half = ff_part // 2
    scale_down = 1.0 / math.sqrt(16 * ff_part)
    scale_b = adapter_scale * scale_right
    tp_index = lax.axis_index("tp")
    rep_index = lax.axis_index("rep")
    zlo, xi = rep_index >> 2, rep_index & 3
    h, y, core = tp_index >> 3, (tp_index >> 1) & 3, tp_index & 1
    side = zlo & 1

    weights = jnp.concatenate([jnp.swapaxes(gate_up, 1, 2), down[None]], axis=0)
    first, second = weights[:, :half], weights[:, half:]
    mine = jnp.where(side == 0, first, second)
    theirs = jnp.where(side == 0, second, first)
    pieces = [mine, rep_xor(theirs, 4)]
    pieces.append(rep_xor(mine, 8))
    pieces.append(rep_xor(pieces[1], 8))

    def after(value, earlier):
        return lax.optimization_barrier((value, earlier))

    live = token_ids != 0
    masked = jnp.where(live[:, None], cotangent, jnp.zeros_like(cotangent))
    wide_cols = width // 8
    column = (tp_index & 7) * wide_cols

    def partner_rows(part):
        right, left, far_first, far_second = ring_gather(part, tp_yshift, 0)
        far = jnp.concatenate([far_first, far_second], axis=0)
        own_core = jnp.stack([part, right, far, left], axis=0)
        other_core = tp_xor(own_core, 1)
        even = jnp.where(core == 0, own_core, other_core)
        odd = jnp.where(core == 0, other_core, own_core)
        return jnp.concatenate([even, odd], axis=2)

    x_send = lax.dynamic_slice_in_dim(tokens, column, wide_cols, 1)
    x_send, pieces[1] = after(x_send, pieces[1])
    x_received = rep_xor(x_send, 4)
    masked_send = lax.dynamic_slice_in_dim(masked, column, wide_cols, 1)
    masked_send, x_received = after(masked_send, x_received)
    masked_received = rep_xor(masked_send, 4)
    x_partner = partner_rows(x_received)
    masked_partner = partner_rows(masked_received)

    wide = wide_side[0]
    hid = hidden_side[0]
    wide_b = wide.astype(BF)
    hid_b = hid.astype(BF)
    hid_first, hid_second = hid_b[:, :, :half], hid_b[:, :, half:]
    hid_mine = jnp.where(side == 0, hid_first, hid_second)
    hid_theirs = jnp.where(side == 0, hid_second, hid_first)

    x_part = lax.dynamic_slice_in_dim(tokens, tp_index * portion, portion, 1)
    masked_part = lax.dynamic_slice_in_dim(masked, tp_index * portion, portion, 1)
    pair_a = wide_b[:2].reshape(2 * adapter_rank, portion)
    start = jnp.concatenate(
        [contract_last(x_part, pair_a), contract_last(masked_part, wide_b[2])], axis=1
    )
    start, pieces[3] = after(start, pieces[3])
    hid_theirs, pieces[3] = after(hid_theirs, pieces[3])
    hid_pair = [hid_mine, rep_xor(hid_theirs, 4)]
    start = tp_sum(start, y, F32)
    low_w = jnp.concatenate(
        [
            (start[:, : 2 * adapter_rank] * scale_left).astype(BF),
            start[:, 2 * adapter_rank :].astype(BF),
        ],
        axis=1,
    )
    low_w_pair = [low_w, rep_xor(low_w, 4)]

    sums = [[None] * 3, [None] * 3]
    for zoff in range(4):
        own = pieces[zoff]
        right, left, far_first, far_second = ring_gather(own, rep_xshift, 1)
        zero = jnp.int32(0)

        def place(buffer, piece, xoff, row):
            col = ((xi + xoff) & 3) * portion
            return lax.dynamic_update_slice(buffer, piece, (zero, jnp.int32(row), col))

        block = jnp.concatenate([own] * 4, axis=2)
        block = place(block, right, 1, 0)
        block = place(block, left, 3, 0)
        block = place(block, far_first, 2, 0)
        block = place(block, far_second, 2, half // 2)
        where_z = zlo ^ zoff
        where_p = (where_z - y) & 3
        rows = [
            [
                lax.dynamic_slice_in_dim(tokens, where_z * 4 * portion, 4 * portion, 1),
                lax.dynamic_slice_in_dim(masked, where_z * 4 * portion, 4 * portion, 1),
            ],
            [
                lax.dynamic_index_in_dim(x_partner, where_p, 0, keepdims=False),
                lax.dynamic_index_in_dim(masked_partner, where_p, 0, keepdims=False),
            ],
        ]
        for q in range(2):
            for k in range(3):
                term = contract_last(rows[q][k // 2], block[k])
                sums[q][k] = term if zoff == 0 else sums[q][k] + term

    partials, grads = [], []
    for q in range(2):
        low_gate = low_w_pair[q][:, :adapter_rank]
        low_up = low_w_pair[q][:, adapter_rank : 2 * adapter_rank]
        weight_right = low_w_pair[q][:, 2 * adapter_rank :]
        hid_q = hid_pair[q]
        gate_values = sums[q][0] + scale_b * matmul(low_gate, hid_q[0])
        up_values = sums[q][1] + scale_b * matmul(low_up, hid_q[1])
        hidden_gradient = sums[q][2] + scale_b * scale_down * matmul(weight_right, hid_q[2])
        sig = jax.nn.sigmoid(gate_values)
        act = gate_values * sig
        hidden_state = (act * up_values).astype(BF)
        gate_gradient = (
            hidden_gradient * up_values * sig * (1.0 + gate_values * (1.0 - sig))
        ).astype(BF)
        up_gradient = (hidden_gradient * act).astype(BF)
        partials.append(
            jnp.concatenate(
                [
                    contract_last(gate_gradient, hid_q[0]),
                    contract_last(up_gradient, hid_q[1]),
                    contract_last(hidden_state, hid_q[2]),
                ],
                axis=1,
            )
        )
        grads.append(
            jnp.stack(
                [
                    scale_b * contract_leading(low_gate, gate_gradient),
                    scale_b * contract_leading(low_up, up_gradient),
                    scale_b * scale_down * contract_leading(weight_right, hidden_state),
                ],
                axis=0,
            )
        )
    partial = partials[0] + rep_xor(partials[1].astype(BF), 4).astype(F32)
    summed = tp_sum(partial, y, BF)
    zsum = summed[:, : 2 * adapter_rank]
    ud = (summed[:, 2 * adapter_rank :].astype(F32) * scale_down).astype(BF)

    grad_other = rep_xor(grads[1].astype(BF), 4).astype(F32)
    grad_hid = jnp.where(
        side == 0,
        jnp.concatenate([grads[0], grad_other], axis=2),
        jnp.concatenate([grad_other, grads[0]], axis=2),
    )
    gradient_down_right = scale_b * contract_leading(ud, masked_part)
    gradient_left = (
        adapter_scale * scale_left * scale_right * contract_leading(zsum, x_part)
    ).reshape(2, adapter_rank, portion)
    grad_wide = jnp.concatenate([gradient_left, gradient_down_right[None]], axis=0)
    wide_new, wmom_new, wvar_new = adam_step(wide, wide_mom[0], wide_var[0], grad_wide)
    hid_new, hmom_new, hvar_new = adam_step(hid, hidden_mom[0], hidden_var[0], grad_hid)

    own_ids = jnp.arange(partner.shape[0], dtype=jnp.int32)
    shift_value = jnp.max(jnp.bitwise_xor(partner, own_ids))
    paired = partner[rep_index] != rep_index

    def swap(value):
        branches = [lambda v: v] + [
            (lambda v, mask=mask: rep_xor(v, mask)) for mask in range(1, 16)
        ]
        return lax.switch(shift_value, branches, value)

    def average(new, received):
        return jnp.where(paired, 0.5 * (new + received.astype(F32)), new)

    wide_final = average(wide_new, swap(wide_new.astype(BF)))
    copy_own = wide_final.astype(BF)
    copy_other = tp_xor(copy_own, 8)
    hid_send, copy_own = after(hid_new.astype(BF), copy_own)
    received_hid, copy_other = after(swap(hid_send), copy_other)
    hid_final = average(hid_new, received_hid)

    both = jnp.stack(
        [jnp.where(h == 0, copy_own, copy_other), jnp.where(h == 0, copy_other, copy_own)], axis=2
    )
    ring = [both] + [tp_yshift(both, 4 - step) for step in (1, 2, 3)]
    ring = jnp.stack(ring + ring[:3], axis=3)
    ring = lax.dynamic_slice_in_dim(ring, (4 - y) & 3, 4, 3)
    ring_other = tp_xor(ring, 1)
    even = jnp.where(core == 0, ring, ring_other)
    odd = jnp.where(core == 0, ring_other, ring)
    wide_copy = jnp.stack([even, odd], axis=4).reshape(3, adapter_rank, 16 * portion)
    return (
        wide_final[None],
        hid_final[None],
        wmom_new[None],
        hmom_new[None],
        wvar_new[None],
        hvar_new[None],
        wide_copy[None],
    )


def solution(mesh):
    side = P("rep", None, None, "tp")
    return jax.shard_map(
        shards,
        mesh=mesh,
        in_specs=(
            P("rep", None),
            P("rep", None),
            P("rep"),
            P(),
            P(None, "rep", "tp"),
            P("tp", "rep"),
            side,
            side,
            side,
            side,
            side,
            side,
        ),
        out_specs=(side, side, side, side, side, side, P("rep", None, None, None)),
        check_vma=False,
    )
```

```python
import math

import jax
import jax.numpy as jnp
from jax import lax
from jax.sharding import PartitionSpec as P


adapter_scale = 0.5
learn_rate = 0.1
beta_one = 0.9
beta_two = 0.99
bias_one = 1.0 - 0.9**10
bias_two = 1.0 - 0.99**10
adam_eps = 1e-08

BF = jnp.bfloat16
F32 = jnp.float32


def rep_xor(value, mask):
    return lax.ppermute(value, "rep", [(r, r ^ mask) for r in range(16)])


def rep_xshift(value, step):
    return lax.ppermute(value, "rep", [(r, (r & 12) | ((r + step) & 3)) for r in range(16)])


def tp_xor(value, mask):
    return lax.ppermute(value, "tp", [(t, t ^ mask) for t in range(16)])


def tp_yshift(value, step):
    return lax.ppermute(
        value, "tp", [(t, (t & 9) | ((((t >> 1) + step) & 3) << 1)) for t in range(16)]
    )


def adam_step(param, moment, second, grad):
    moment_new = beta_one * moment + (1.0 - beta_one) * grad
    second_new = beta_two * second + (1.0 - beta_two) * grad * grad
    param_new = param - learn_rate * (moment_new / bias_one) / (
        jnp.sqrt(second_new / bias_two) + adam_eps
    )
    return (param_new, moment_new, second_new)


def contract_last(left, right):
    return lax.dot_general(
        left, right, (((1,), (1,)), ((), ())), preferred_element_type=F32
    )


def contract_leading(left, right):
    return lax.dot_general(
        left, right, (((0,), (0,)), ((), ())), preferred_element_type=F32
    )


def matmul(left, right):
    return jnp.dot(left, right, preferred_element_type=F32)


def tp_sum(part, y, wire, hold=lambda v: v):
    rows = part.shape[0] // 4
    part = part + tp_xor(part.astype(wire), 1).astype(F32)

    def quarter(index):
        return lax.dynamic_slice_in_dim(part, (index & 3) * rows, rows, 0)

    total = quarter(y)
    for step in (1, 3, 2):
        total = total + tp_yshift(quarter(y + step).astype(wire), step).astype(F32)
    total = (total + hold(tp_xor(total.astype(wire), 8)).astype(F32)).astype(wire)
    pieces = [total] + [tp_yshift(total, 4 - step) for step in (1, 2, 3)]
    joined = jnp.concatenate(pieces + pieces[:3], axis=0)
    return lax.dynamic_slice_in_dim(joined, ((4 - y) & 3) * rows, 4 * rows, 0)


def ring_gather(own, shift, axis):
    half = own.shape[axis] // 2
    right = shift(own, -1)
    left = shift(own, 1)
    far_first = shift(lax.slice_in_dim(left, 0, half, axis=axis), 1)
    far_second = shift(lax.slice_in_dim(right, half, 2 * half, axis=axis), -1)
    return right, left, far_first, far_second


def shards(
    tokens,
    cotangent,
    token_ids,
    partner,
    gate_up,
    down,
    wide_side,
    hidden_side,
    wide_mom,
    hidden_mom,
    wide_var,
    hidden_var,
):
    width = tokens.shape[1]
    adapter_rank = wide_side.shape[2]
    portion = wide_side.shape[3]
    scale_left = 1.0 / math.sqrt(width)
    scale_right = 1.0 / math.sqrt(adapter_rank)
    ff_part = down.shape[0]
    half = ff_part // 2
    scale_down = 1.0 / math.sqrt(16 * ff_part)
    scale_b = adapter_scale * scale_right
    tp_index = lax.axis_index("tp")
    rep_index = lax.axis_index("rep")
    zlo, xi = rep_index >> 2, rep_index & 3
    h, y, core = tp_index >> 3, (tp_index >> 1) & 3, tp_index & 1
    side = zlo & 1

    weights = jnp.concatenate([jnp.swapaxes(gate_up, 1, 2), down[None]], axis=0)
    first, second = weights[:, :half], weights[:, half:]
    mine = jnp.where(side == 0, first, second)
    theirs = jnp.where(side == 0, second, first)
    pieces = [mine, rep_xor(theirs, 4)]
    pieces.append(rep_xor(mine, 8))
    pieces.append(rep_xor(pieces[1], 8))

    def after(value, earlier):
        return lax.optimization_barrier((value, earlier))

    live = token_ids != 0
    masked = jnp.where(live[:, None], cotangent, jnp.zeros_like(cotangent))
    wide_cols = width // 8
    column = (tp_index & 7) * wide_cols

    def partner_rows(part):
        right, left, far_first, far_second = ring_gather(part, tp_yshift, 0)
        far = jnp.concatenate([far_first, far_second], axis=0)
        own_core = jnp.stack([part, right, far, left], axis=0)
        other_core = tp_xor(own_core, 1)
        even = jnp.where(core == 0, own_core, other_core)
        odd = jnp.where(core == 0, other_core, own_core)
        return jnp.concatenate([even, odd], axis=2)

    x_send = lax.dynamic_slice_in_dim(tokens, column, wide_cols, 1)
    x_send, pieces[1] = after(x_send, pieces[1])
    x_received = rep_xor(x_send, 4)
    masked_send = lax.dynamic_slice_in_dim(masked, column, wide_cols, 1)
    masked_send, x_received = after(masked_send, x_received)
    masked_received = rep_xor(masked_send, 4)
    x_partner = partner_rows(x_received)
    masked_partner = partner_rows(masked_received)

    wide = wide_side[0]
    hid = hidden_side[0]
    wide_b = wide.astype(BF)
    hid_b = hid.astype(BF)
    hid_first, hid_second = hid_b[:, :, :half], hid_b[:, :, half:]
    hid_mine = jnp.where(side == 0, hid_first, hid_second)
    hid_theirs = jnp.where(side == 0, hid_second, hid_first)

    x_part = lax.dynamic_slice_in_dim(tokens, tp_index * portion, portion, 1)
    masked_part = lax.dynamic_slice_in_dim(masked, tp_index * portion, portion, 1)
    pair_a = wide_b[:2].reshape(2 * adapter_rank, portion)
    start = jnp.concatenate(
        [contract_last(x_part, pair_a), contract_last(masked_part, wide_b[2])], axis=1
    )
    hid_theirs, pieces[3] = after(hid_theirs, pieces[3])
    hid_pair = [hid_mine, rep_xor(hid_theirs, 4)]

    def hold(received):
        received, pieces[2] = after(received, pieces[2])
        return received

    start = tp_sum(start, y, F32, hold)
    low_w = jnp.concatenate(
        [
            (start[:, : 2 * adapter_rank] * scale_left).astype(BF),
            start[:, 2 * adapter_rank :].astype(BF),
        ],
        axis=1,
    )
    low_w_pair = [low_w, rep_xor(low_w, 4)]

    sums = [[None] * 3, [None] * 3]
    for zoff in range(4):
        own = pieces[zoff]
        right, left, far_first, far_second = ring_gather(own, rep_xshift, 1)
        zero = jnp.int32(0)

        def place(buffer, piece, xoff, row):
            col = ((xi + xoff) & 3) * portion
            return lax.dynamic_update_slice(buffer, piece, (zero, jnp.int32(row), col))

        block = jnp.concatenate([own] * 4, axis=2)
        block = place(block, right, 1, 0)
        block = place(block, left, 3, 0)
        block = place(block, far_first, 2, 0)
        block = place(block, far_second, 2, half // 2)
        where_z = zlo ^ zoff
        where_p = (where_z - y) & 3
        rows = [
            [
                lax.dynamic_slice_in_dim(tokens, where_z * 4 * portion, 4 * portion, 1),
                lax.dynamic_slice_in_dim(masked, where_z * 4 * portion, 4 * portion, 1),
            ],
            [
                lax.dynamic_index_in_dim(x_partner, where_p, 0, keepdims=False),
                lax.dynamic_index_in_dim(masked_partner, where_p, 0, keepdims=False),
            ],
        ]
        for q in range(2):
            for k in range(3):
                term = contract_last(rows[q][k // 2], block[k])
                sums[q][k] = term if zoff == 0 else sums[q][k] + term

    partials, grads = [], []
    for q in range(2):
        low_gate = low_w_pair[q][:, :adapter_rank]
        low_up = low_w_pair[q][:, adapter_rank : 2 * adapter_rank]
        weight_right = low_w_pair[q][:, 2 * adapter_rank :]
        hid_q = hid_pair[q]
        gate_values = sums[q][0] + scale_b * matmul(low_gate, hid_q[0])
        up_values = sums[q][1] + scale_b * matmul(low_up, hid_q[1])
        hidden_gradient = sums[q][2] + scale_b * scale_down * matmul(weight_right, hid_q[2])
        sig = jax.nn.sigmoid(gate_values)
        act = gate_values * sig
        hidden_state = (act * up_values).astype(BF)
        gate_gradient = (
            hidden_gradient * up_values * sig * (1.0 + gate_values * (1.0 - sig))
        ).astype(BF)
        up_gradient = (hidden_gradient * act).astype(BF)
        partials.append(
            jnp.concatenate(
                [
                    contract_last(gate_gradient, hid_q[0]),
                    contract_last(up_gradient, hid_q[1]),
                    contract_last(hidden_state, hid_q[2]),
                ],
                axis=1,
            )
        )
        grads.append(
            jnp.stack(
                [
                    scale_b * contract_leading(low_gate, gate_gradient),
                    scale_b * contract_leading(low_up, up_gradient),
                    scale_b * scale_down * contract_leading(weight_right, hidden_state),
                ],
                axis=0,
            )
        )
    partial = partials[0] + rep_xor(partials[1].astype(BF), 4).astype(F32)
    summed = tp_sum(partial, y, BF)
    zsum = summed[:, : 2 * adapter_rank]
    ud = (summed[:, 2 * adapter_rank :].astype(F32) * scale_down).astype(BF)

    grad_other = rep_xor(grads[1].astype(BF), 4).astype(F32)
    grad_hid = jnp.where(
        side == 0,
        jnp.concatenate([grads[0], grad_other], axis=2),
        jnp.concatenate([grad_other, grads[0]], axis=2),
    )
    gradient_down_right = scale_b * contract_leading(ud, masked_part)
    gradient_left = (
        adapter_scale * scale_left * scale_right * contract_leading(zsum, x_part)
    ).reshape(2, adapter_rank, portion)
    grad_wide = jnp.concatenate([gradient_left, gradient_down_right[None]], axis=0)
    wide_new, wmom_new, wvar_new = adam_step(wide, wide_mom[0], wide_var[0], grad_wide)
    hid_new, hmom_new, hvar_new = adam_step(hid, hidden_mom[0], hidden_var[0], grad_hid)

    own_ids = jnp.arange(partner.shape[0], dtype=jnp.int32)
    shift_value = jnp.max(jnp.bitwise_xor(partner, own_ids))
    paired = partner[rep_index] != rep_index

    def swap(value):
        branches = [lambda v: v] + [
            (lambda v, mask=mask: rep_xor(v, mask)) for mask in range(1, 16)
        ]
        return lax.switch(shift_value, branches, value)

    def average(new, received):
        return jnp.where(paired, 0.5 * (new + received.astype(F32)), new)

    wide_final = average(wide_new, swap(wide_new.astype(BF)))
    copy_own = wide_final.astype(BF)
    copy_other = tp_xor(copy_own, 8)
    hid_send, copy_own = after(hid_new.astype(BF), copy_own)
    received_hid, copy_other = after(swap(hid_send), copy_other)
    hid_final = average(hid_new, received_hid)

    both = jnp.stack(
        [jnp.where(h == 0, copy_own, copy_other), jnp.where(h == 0, copy_other, copy_own)], axis=2
    )
    ring = [both] + [tp_yshift(both, 4 - step) for step in (1, 2, 3)]
    ring = jnp.stack(ring + ring[:3], axis=3)
    ring = lax.dynamic_slice_in_dim(ring, (4 - y) & 3, 4, 3)
    ring_other = tp_xor(ring, 1)
    even = jnp.where(core == 0, ring, ring_other)
    odd = jnp.where(core == 0, ring_other, ring)
    wide_copy = jnp.stack([even, odd], axis=4).reshape(3, adapter_rank, 16 * portion)
    return (
        wide_final[None],
        hid_final[None],
        wmom_new[None],
        hmom_new[None],
        wvar_new[None],
        hvar_new[None],
        wide_copy[None],
    )


def solution(mesh):
    side = P("rep", None, None, "tp")
    return jax.shard_map(
        shards,
        mesh=mesh,
        in_specs=(
            P("rep", None),
            P("rep", None),
            P("rep"),
            P(),
            P(None, "rep", "tp"),
            P("tp", "rep"),
            side,
            side,
            side,
            side,
            side,
            side,
        ),
        out_specs=(side, side, side, side, side, side, P("rep", None, None, None)),
        check_vma=False,
    )
```
